128 devices in a mesh: ctx: 8 (over z_hi, x), tp: 8 (over y, core), dp: 2 (over z_lo).
Axes of the slice: x: 4, y: 4, z: 4 (z_hi: 2, z_lo: 2; z = z_hi * 2 + z_lo), core: 2. Of those that a mesh axis runs over, the one named last changes fastest.
Arguments:
- queries: bfloat16 [2, 4096, 8192], P('dp', 'ctx', 'tp'), may hold values from -80 to 80, as said below
- keys: bfloat16 [2, 4096, 8192], P('dp', 'ctx', 'tp'), may hold values from -4 to 4
- values: bfloat16 [2, 4096, 8192], P('dp', 'ctx', 'tp'), may hold values from -6 to 6
- bias_u: float32 [8192], P('tp'), may hold values from -3 to 3
- bias_w: float32 [8192], P('tp'), may hold values from -3 to 3
- rel_table: bfloat16 [1024, 8192], P(None, 'tp'), may hold values from -1.1953125 to 1.1953125
- out_weight: bfloat16 [8192, 8192], P('tp', ('ctx', 'dp')), may hold values from -0.0625 to 0.0625
- grad_out: bfloat16 [2, 4096, 8192], P('dp', 'ctx', 'tp'), may hold values from -6 to 6
- doc_lengths: int32 [2, 16], P('dp'), may hold values from 1 to 1024, 4096 in all within a row
Outputs:
- grad_queries: bfloat16 [2, 4096, 8192], P('dp', 'ctx', 'tp')
- grad_keys: bfloat16 [2, 4096, 8192], P('dp', 'ctx', 'tp')
- grad_values: bfloat16 [2, 4096, 8192], P('dp', 'ctx', 'tp')
- grad_table: float32 [1024, 8192], P(None, 'tp')
- grad_biases: float32 [2, 8192], P(None, 'tp')
The draws below stay inside these ranges and needn't reach their ends.
Inputs may be any that keep to these rules, and one draw needn't show every extreme that they name: Entries of keys lie within the range; row t of a head's queries may be a multiple, up to 20, of its key row t. `doc_lengths`: each row's 16 lengths sum to 4096, and the longest document in each row has 1024 tokens.
All inputs are finite; a program needn't handle non-finite values.
Results may differ from the reference program's by a relative error of at most 0.0074.
Values may be sent and summed in bfloat16 or wider, within the bound.
No kernel may reach another device: no remote copies, remote signals or barrier semaphores. Data moves between devices by JAX's collectives and lax.ppermute only.
A program may use at most 192 MiB of HBM per device.

```python
import math
import jax
import jax.numpy as jnp
import numpy as np
from jax import lax

D = 8192
HEADS = 64
HD = 128
SEG = 512
HH = 8192
STREAMS = 2
TOKENS = 4096
DOCS = 16
DOC_MOST = 1024
RELS = 1024
N_CTX = 8


def draw_pair(key):
    base = jax.random.fold_in(key, 7)
    key_first, key_second = jax.random.split(base, 2)
    shape = (STREAMS, TOKENS, HEADS * HD)
    keys_raw = jnp.clip(jax.random.normal(key_first, shape, jnp.float32), -4.0, 4.0)
    query_raw = jnp.clip(jax.random.normal(key_second, shape, jnp.float32), -4.0, 4.0)
    return (query_raw, keys_raw)


def draw_queries(key, part):
    return draw_pair(key)[0].astype(jnp.bfloat16)


def draw_keys(key, part):
    return draw_pair(key)[1].astype(jnp.bfloat16)


def shard_levels(own_key, dims, shards, least, high):
    def one(axis_at, parts):
        heights = jax.random.uniform(jax.random.fold_in(jax.random.fold_in(own_key, 6), axis_at), (parts,), jnp.float32, least / len(shards), high / len(shards))
        return jnp.repeat(jnp.exp(heights), dims[axis_at] // parts).reshape((-1,) + (1,) * (len(dims) - axis_at - 1))

    level = one(*shards[0])
    for cut in shards[1:]:
        level = level * one(*cut)
    return level


def length_profile(amount, total, most, slope):
    portions = [(1 << 20) // math.isqrt(grade ** slope) + 1 for grade in range(2, amount + 1)]
    rest, given = total - most - (amount - 1), [1] * (amount - 1)
    while rest > 0:
        free = [i for i in range(amount - 1) if given[i] < most]
        mass, left = sum([portions[i] for i in free]), rest
        for i in free:
            addition = min(most - given[i], max(1, left * portions[i] // mass), rest)
            given[i] = given[i] + addition
            rest = rest - addition
    return np.array([most] + given)


def uneven_parts(key, count, total, most, skew):
    if count == 2:
        one = jax.random.randint(key, (), max(1, total - most), min(most, total - 1) + 1)
        return jnp.stack([one, total - one])
    lengths = jnp.asarray(length_profile(count, total, most, skew), jnp.int32)
    twos = (count - 1) // 2
    donor, receiver = lengths[1:1 + 2 * twos:2], lengths[2:2 + 2 * twos:2]
    slack = jnp.minimum(donor - 1, most - receiver)
    passed = jax.random.randint(jax.random.fold_in(key, 1), (twos,), 0, 1 << 20) % (slack + 1)
    lengths = lengths.at[1:1 + 2 * twos:2].set(donor - passed).at[2:2 + 2 * twos:2].set(receiver + passed)
    return lengths[jax.random.permutation(jax.random.fold_in(key, 2), count)]


def bell_draw(stream_key, dims, spread, most, cuts=(), held_as=jnp.bfloat16):
    drawn = spread * jax.random.normal(stream_key, dims, jnp.float32)
    if cuts:
        drawn = drawn * shard_levels(stream_key, dims, cuts, -0.22, 0.18)
    return jnp.clip(drawn, -most, most).astype(held_as)


def setup_inputs(seed: int = 0) -> dict:
    splits = jax.random.split(jax.random.key(seed), 10)
    queries = draw_queries(jax.random.fold_in(splits[9], 71), 0)
    keys = draw_keys(jax.random.fold_in(splits[9], 71), 0)
    values = bell_draw(splits[2], (STREAMS, TOKENS, HH), 1.0, 6.0, ((0, 2), (1, 8), (2, 8)))
    bias_u = bell_draw(splits[3], (HH,), 0.5, 3.0, ((0, 8),), jnp.float32)
    bias_w = bell_draw(splits[4], (HH,), 0.5, 3.0, ((0, 8),), jnp.float32)
    rel_table = bell_draw(splits[5], (RELS, HH), 0.2, 1.1953125, ((1, 8),))
    out_weight = bell_draw(splits[6], (HH, D), HH ** -0.5, 0.0625, ((0, 8), (1, 16)))
    grad_out = bell_draw(splits[7], (STREAMS, TOKENS, D), 1.0, 6.0, ((0, 2), (1, 8), (2, 8)))
    doc_lengths = jax.vmap(lambda own: uneven_parts(own, DOCS, TOKENS, DOC_MOST, 2))(jax.random.split(splits[8], STREAMS)).reshape((STREAMS, DOCS)).astype(jnp.int32)
    return dict(queries=queries, keys=keys, values=values, bias_u=bias_u, bias_w=bias_w, rel_table=rel_table, out_weight=out_weight, grad_out=grad_out, doc_lengths=doc_lengths)


def sequence_head(query_rows, key_rows, value_rows, grad_rows, bias_u_row, bias_w_row, rel_rows, doc_ids):
    blocks = N_CTX
    score_scale = 1.0 / math.sqrt(HD)
    query_blocks = query_rows.reshape(blocks, SEG, HD)
    key_blocks = key_rows.reshape(blocks, SEG, HD)
    value_blocks = value_rows.reshape(blocks, SEG, HD)
    grad_blocks = grad_rows.reshape(blocks, SEG, HD)
    empty = jnp.zeros((1, SEG, HD), key_rows.dtype)
    keys_all = jnp.concatenate([jnp.concatenate([empty, key_blocks[:-1]], axis=0), key_blocks], axis=1)
    values_all = jnp.concatenate([jnp.concatenate([empty, value_blocks[:-1]], axis=0), value_blocks], axis=1)
    positions = jnp.arange(blocks * SEG, dtype=jnp.int32).reshape(blocks, SEG)
    doc_blocks = doc_ids.reshape(blocks, SEG)
    doc_keys = jnp.concatenate([jnp.concatenate([jnp.full((1, SEG), -1, jnp.int32), doc_blocks[:-1]], axis=0), doc_blocks], axis=1)
    key_pos = jnp.concatenate([positions - SEG, positions], axis=1)
    row_ids = jnp.arange(SEG, dtype=jnp.int32)[:, None]
    col_ids = jnp.arange(2 * SEG, dtype=jnp.int32)[None, :]
    visible = (key_pos[:, None, :] >= 0) & (col_ids <= row_ids + SEG)[None] & (doc_keys[:, None, :] == doc_blocks[:, :, None])
    query_content = (query_blocks.astype(jnp.float32) + bias_u_row).astype(jnp.bfloat16)
    query_position = (query_blocks.astype(jnp.float32) + bias_w_row).astype(jnp.bfloat16)
    content = jnp.einsum('cid,cjd->cij', query_content.astype(jnp.float32), keys_all.astype(jnp.float32))
    rel_raw = jnp.einsum('cid,ed->cie', query_position.astype(jnp.float32), rel_rows.astype(jnp.float32))
    distance = jnp.clip(row_ids + SEG - col_ids, 0, 2 * SEG - 1).astype(jnp.int32)
    rel_term = jnp.take_along_axis(rel_raw, jnp.broadcast_to(distance[None], (blocks, SEG, 2 * SEG)), axis=2)
    logits = jnp.where(visible, (content + rel_term) * score_scale, -jnp.inf)
    row_peak = lax.optimization_barrier(jnp.max(logits, axis=2, keepdims=True))
    raised = jnp.exp(logits - row_peak)
    weights = raised / lax.optimization_barrier(jnp.sum(raised, axis=2, keepdims=True))
    grad_weights = jnp.einsum('cid,cjd->cij', grad_blocks.astype(jnp.float32), values_all.astype(jnp.float32))
    row_inner = lax.optimization_barrier(jnp.sum(weights * grad_weights, axis=2, keepdims=True))
    grad_logits = (weights * (grad_weights - row_inner) * score_scale).astype(jnp.bfloat16)
    weights_low = weights.astype(jnp.bfloat16)
    source = row_ids + SEG - col_ids
    source_ok = (source >= 0) & (source < 2 * SEG)
    source_idx = jnp.clip(source, 0, 2 * SEG - 1).astype(jnp.int32)
    grad_shifted = jnp.where(source_ok[None], jnp.take_along_axis(grad_logits, jnp.broadcast_to(source_idx[None], (blocks, SEG, 2 * SEG)), axis=2), jnp.zeros((), jnp.bfloat16))
    grad_logits_wide = grad_logits.astype(jnp.float32)
    grad_shifted_wide = grad_shifted.astype(jnp.float32)
    query_content_part = jnp.einsum('cij,cjd->cid', grad_logits_wide, keys_all.astype(jnp.float32))
    query_rel_part = jnp.einsum('cie,ed->cid', grad_shifted_wide, rel_rows.astype(jnp.float32))
    grad_query = (query_content_part + query_rel_part).astype(jnp.bfloat16).reshape(blocks * SEG, HD)
    grad_keys_all = jnp.einsum('cij,cid->cjd', grad_logits_wide, query_content.astype(jnp.float32))
    grad_values_all = jnp.einsum('cij,cid->cjd', weights_low.astype(jnp.float32), grad_blocks.astype(jnp.float32))
    zero_block = jnp.zeros((1, SEG, HD), jnp.float32)
    grad_key = grad_keys_all[:, SEG:] + jnp.concatenate([grad_keys_all[1:, :SEG], zero_block], axis=0)
    grad_value = grad_values_all[:, SEG:] + jnp.concatenate([grad_values_all[1:, :SEG], zero_block], axis=0)
    grad_rel = jnp.einsum('cie,cid->ed', grad_shifted_wide, query_position.astype(jnp.float32))
    grad_u = lax.optimization_barrier(jnp.sum(query_content_part, axis=(0, 1)))
    grad_w = lax.optimization_barrier(jnp.sum(query_rel_part, axis=(0, 1)))
    return (grad_query, grad_key.astype(jnp.bfloat16).reshape(blocks * SEG, HD), grad_value.astype(jnp.bfloat16).reshape(blocks * SEG, HD), grad_rel, grad_u, grad_w)

def split_heads(rows):
    return rows.reshape(rows.shape[0], HEADS, HD).transpose(1, 0, 2)

def join_heads(stacked):
    return stacked.transpose(1, 0, 2).reshape(stacked.shape[1], HEADS * HD)

def reference(queries, keys, values, bias_u, bias_w, rel_table, out_weight, grad_out, doc_lengths):
    rel_heads = split_heads(rel_table)
    bias_u_heads = bias_u.reshape(HEADS, HD)
    bias_w_heads = bias_w.reshape(HEADS, HD)
    query_list = []
    key_list = []
    value_list = []
    grad_table = jnp.zeros((RELS, HEADS * HD), jnp.float32)
    grad_u_total = jnp.zeros((HEADS * HD,), jnp.float32)
    grad_w_total = jnp.zeros((HEADS * HD,), jnp.float32)
    for sequence in range(STREAMS):
        grad_heads = jnp.dot(grad_out[sequence], out_weight.T, preferred_element_type=jnp.float32).astype(jnp.bfloat16)
        doc_ends = jnp.cumsum(doc_lengths[sequence])
        token_pos = jnp.arange(TOKENS, dtype=jnp.int32)
        doc_ids = lax.optimization_barrier(jnp.sum((doc_ends[None, :] <= token_pos[:, None]).astype(jnp.int32), axis=1))

        def one_head(packed):
            return sequence_head(packed[0], packed[1], packed[2], packed[3], packed[4], packed[5], packed[6], doc_ids)
        results = lax.map(one_head, (split_heads(queries[sequence]), split_heads(keys[sequence]), split_heads(values[sequence]), split_heads(grad_heads), bias_u_heads, bias_w_heads, rel_heads))
        query_list.append(join_heads(results[0]))
        key_list.append(join_heads(results[1]))
        value_list.append(join_heads(results[2]))
        grad_table = grad_table + join_heads(results[3])
        grad_u_total = grad_u_total + results[4].reshape(-1)
        grad_w_total = grad_w_total + results[5].reshape(-1)
    grad_biases = jnp.stack([grad_u_total, grad_w_total])
    return (jnp.stack(query_list), jnp.stack(key_list), jnp.stack(value_list), grad_table, grad_biases)
```

```python
import functools
import math

import jax
import jax.numpy as jnp
from jax import lax
from jax.experimental import pallas as pl
from jax.experimental.pallas import tpu as pltpu
from jax.sharding import Mesh
from jax.sharding import PartitionSpec as P

HD = 128
SCALE = 1.0 / math.sqrt(HD)


def dot_nt(a, b):
    return lax.dot_general(a, b, (((1,), (1,)), ((), ())), preferred_element_type=jnp.float32)


def dot_nn(a, b):
    return lax.dot_general(a, b, (((1,), (0,)), ((), ())), preferred_element_type=jnp.float32)


def dot_tn(a, b):
    return lax.dot_general(a, b, (((0,), (0,)), ((), ())), preferred_element_type=jnp.float32)


def exchange(block=256):
    i = lax.broadcasted_iota(jnp.int32, (block, block), 0)
    j = lax.broadcasted_iota(jnp.int32, (block, block), 1)
    return jnp.where(i + j == block - 1, 1.0, 0.0).astype(jnp.bfloat16)


def flipped_lanes(x, anti):
    block = anti.shape[0]
    n = x.shape[1] // block
    parts = [dot_nn(x[:, k * block:(k + 1) * block], anti) for k in range(n)]
    return jnp.concatenate(parts[::-1], axis=1)


def flipped(rows, block=256):
    n = rows.shape[0] // block
    anti = exchange(block)
    parts = [dot_nn(anti, rows[k * block:(k + 1) * block]) for k in range(n)]
    return jnp.concatenate(parts[::-1], axis=0).astype(jnp.bfloat16)


def weights_body(start, q, k_mem, k_own, rel, bu, bw, w_out, *, block):
    seg = q.shape[0]
    rel_back = flipped(rel[...])
    q32 = q[...].astype(jnp.float32)
    qc = (q32 + bu[...]).astype(jnp.bfloat16)
    qp = (q32 + bw[...]).astype(jnp.bfloat16)
    for r in range(seg // block):
        rows = slice(r * block, (r + 1) * block)
        own = (r + 1) * block
        width = seg + own
        content = jnp.concatenate(
            [dot_nt(qc[rows], k_mem[...]), dot_nt(qc[rows], k_own[:own])], axis=1)
        raw = dot_nt(qp[rows], rel_back[seg - own:])
        raw = pltpu.roll(raw, width - block + 1, 1, stride=1, stride_axis=0)
        col = lax.broadcasted_iota(jnp.int32, (block, width), 1)
        row = lax.broadcasted_iota(jnp.int32, (block, 1), 0)
        seen = (col >= start[rows]) & (col <= row + (r * block + seg))
        logits = jnp.where(seen, (content + raw) * SCALE, -jnp.inf)
        peak = jnp.max(logits, axis=1, keepdims=True)
        raised = jnp.exp(logits - peak)
        w_out[0, rows, :width] = raised / jnp.sum(raised, axis=1, keepdims=True)


def grads_body(w, g, q, k_mem, k_own, v_mem, v_own, rel, bu, bw,
               dq_out, dk_mem, dk_own, dv_mem, dv_own, drel_out, bias_out,
               dk_acc, dv_acc, dr_acc, *, block):
    seg = q.shape[0]
    q32 = q[...].astype(jnp.float32)
    qc = (q32 + bu[...]).astype(jnp.bfloat16)
    qp = (q32 + bw[...]).astype(jnp.bfloat16)
    sum_u = sum_w = 0.0
    nblk = seg // block
    anti = exchange()
    for r in reversed(range(nblk)):
        rows = slice(r * block, (r + 1) * block)
        own = (r + 1) * block
        width = seg + own
        dw = jnp.concatenate(
            [dot_nt(g[rows], v_mem[...]), dot_nt(g[rows], v_own[:own])], axis=1)
        wr = w[0, rows, :width]
        inner = jnp.sum(wr * dw, axis=1, keepdims=True)
        gl32 = wr * (dw - inner) * SCALE
        gl = gl32.astype(jnp.bfloat16)
        gs = pltpu.roll(flipped_lanes(gl, anti), width - block + 1, 1, stride=1, stride_axis=0)
        gs = gs.astype(jnp.bfloat16)
        wl = wr.astype(jnp.bfloat16)
        part_u = dot_nn(gl[:, :seg], k_mem[...]) + dot_nn(gl[:, seg:], k_own[:own])
        part_w = dot_nn(gs, rel[:width])
        dq_out[rows] = (part_u + part_w).astype(jnp.bfloat16)
        sum_u = sum_u + jnp.sum(part_u, axis=0, keepdims=True)
        sum_w = sum_w + jnp.sum(part_w, axis=0, keepdims=True)
        dk = dot_tn(gl, qc[rows])
        dv = dot_tn(wl, g[rows])
        dr = dot_tn(gs, qp[rows])
        if r == nblk - 1:
            dk_acc[...] = dk
            dv_acc[...] = dv
            dr_acc[...] = dr
        else:
            dk_acc[:width] = dk_acc[:width] + dk
            dv_acc[:width] = dv_acc[:width] + dv
            dr_acc[:width] = dr_acc[:width] + dr
    dk_mem[...] = dk_acc[:seg].astype(dk_mem.dtype)
    dk_own[...] = dk_acc[seg:]
    dv_mem[...] = dv_acc[:seg].astype(dv_mem.dtype)
    dv_own[...] = dv_acc[seg:]
    drel_out[...] = dr_acc[...].astype(jnp.bfloat16)
    bias_out[0:1, :] = sum_u
    bias_out[1:2, :] = sum_w


def weights_call(start, q, k_mem, k_own, rel, bu, bw, h0=0, heads=8, block=256):
    seg = q.shape[0]
    rels = rel.shape[0]
    col = lambda n: pl.BlockSpec((n, HD), lambda h: (0, h + h0))
    out = lambda n: pl.BlockSpec((n, HD), lambda h: (0, h))
    return pl.pallas_call(
        functools.partial(weights_body, block=block),
        grid=(heads,),
        in_specs=[pl.BlockSpec((seg, 1), lambda h: (0, 0)), col(seg), col(seg), col(seg), col(rels), col(1), col(1)],
        out_specs=pl.BlockSpec((1, seg, 2 * seg), lambda h: (h, 0, 0)),
        out_shape=jax.ShapeDtypeStruct((heads, seg, 2 * seg), jnp.float32),
        name="attn_weights",
    )(start, q, k_mem, k_own, rel, bu, bw)


def grads_call(w, g, q, k_mem, k_own, v_mem, v_own, rel, bu, bw, h0=0, heads=8, block=256):
    seg = q.shape[0]
    rels = rel.shape[0]
    col = lambda n: pl.BlockSpec((n, HD), lambda h: (0, h + h0))
    out = lambda n: pl.BlockSpec((n, HD), lambda h: (0, h))
    f = lambda n, dt: jax.ShapeDtypeStruct((n, heads * HD), dt)
    bf, f32 = jnp.bfloat16, jnp.float32
    return pl.pallas_call(
        functools.partial(grads_body, block=block),
        grid=(heads,),
        in_specs=[pl.BlockSpec((1, seg, 2 * seg), lambda h: (h + h0, 0, 0)), out(seg), col(seg), col(seg), col(seg),
                  col(seg), col(seg), col(rels), col(1), col(1)],
        out_specs=[out(seg)] * 5 + [out(rels), out(2)],
        out_shape=[f(seg, bf), f(seg, bf), f(seg, f32), f(seg, bf), f(seg, f32), f(rels, bf), f(2, f32)],
        scratch_shapes=[pltpu.VMEM((rels, HD), f32)] * 3,
        name="attn_grads",
    )(w, g, q, k_mem, k_own, v_mem, v_own, rel, bu, bw)


AXES = ("zh", "x", "y", "co", "zl")
CTX = ("zh", "x")
Z = ("zh", "zl")
TP = ("y", "co")
CTX_DP = ("zh", "x", "zl")
NEAR = (0, -1, 1, 2)


def hop(value, axis, steps):
    count = lax.axis_size(axis)
    return lax.ppermute(value, axis, [(i, (i + steps) % count) for i in range(count)])


def from_behind(value, axis, steps):
    count = lax.axis_size(axis)
    first, last = (max(0, -steps), min(count, count - steps))
    return lax.ppermute(value, axis, [(i, i + steps) for i in range(first, last)])


def ring_gather(own, axis):
    half = own.shape[0] // 2
    behind = hop(own, axis, 1)
    ahead = hop(own, axis, -1)
    return behind, ahead, hop(behind[:half], axis, 1), hop(ahead[half:], axis, -1)


def stacked_ring(own, axis):
    behind, ahead, far_low, far_high = ring_gather(own, axis)
    return jnp.stack([own, behind, ahead, jnp.concatenate([far_low, far_high], axis=0)])


def two_axes(own, first, second):
    near = stacked_ring(own, first)
    return (near,) + ring_gather(near, second)


def project_body(slices, blocks, w0, w1, w2, w3, w4, cot_own, cot_side, out, cot, wbuf, acc, cot_sem, w_sem):
    parts = [(ref, i) for ref in (w0, w1, w2, w3, w4) for i in range(ref.shape[0])]
    depth = wbuf.shape[0]
    wide = cot.shape[2]

    def w_copy(k):
        ref, i = parts[k]
        return pltpu.make_async_copy(ref.at[i], wbuf.at[k % depth], w_sem.at[k % depth])

    for k in range(depth - 1):
        w_copy(k).start()
    cot_copies = []
    for side, ref in enumerate((cot_own, cot_side)):
        for i in range(ref.shape[0]):
            for part in range(2):
                block = blocks[side * ref.shape[0] + i] * 2 + part
                cot_copies.append(pltpu.make_async_copy(
                    ref.at[i, :, pl.ds(part * wide, wide)], cot.at[block], cot_sem.at[side, i, part]))
    for copy in cot_copies:
        copy.start()
    for copy in cot_copies:
        copy.wait()
    for k in range(len(parts)):
        if k + depth - 1 < len(parts):
            w_copy(k + depth - 1).start()
        w_copy(k).wait()
        product = dot_nt(cot[slices[k]], wbuf[k % depth])
        if k == 0:
            acc[...] = product
        elif k < len(parts) - 1:
            acc[...] = acc[...] + product
        else:
            out[...] = (acc[...] + product).astype(out.dtype)


def project(slices, blocks, pieces, cot_own, cot_side):
    rows, depth = pieces[0].shape[1:]
    tokens = cot_own.shape[1]
    return pl.pallas_call(
        project_body,
        in_specs=[pl.BlockSpec(memory_space=pltpu.SMEM)] * 2 + [pl.BlockSpec(memory_space=pl.ANY)] * 7,
        out_shape=jax.ShapeDtypeStruct((tokens, rows), jnp.bfloat16),
        scratch_shapes=[
            pltpu.VMEM((16, tokens, depth), jnp.bfloat16),
            pltpu.VMEM((4, rows, depth), jnp.bfloat16),
            pltpu.VMEM((tokens, rows), jnp.float32),
            pltpu.SemaphoreType.DMA((2, 4, 2)),
            pltpu.SemaphoreType.DMA((4,)),
        ],
        cost_estimate=pl.CostEstimate(
            flops=2 * tokens * rows * depth * 16, bytes_accessed=2 * (16 * rows * depth + 16 * tokens * depth),
            transcendentals=0),
        name="project",
    )(slices, blocks, *pieces, cot_own, cot_side)


def block_of(value, index, count):
    rows = value.shape[0] // count
    return lax.dynamic_slice_in_dim(value, (index % count) * rows, rows, 0)


def scatter_sum(value, axis):
    here = lax.axis_index(axis)
    own = block_of(value, here, 4).astype(jnp.float32)
    got = [hop(block_of(value, here + k, 4), axis, k).astype(jnp.float32) for k in (1, 3, 2)]
    return ((own + got[2]) + (got[0] + got[1])).astype(value.dtype)


def gather_rows(block, axis):
    here = lax.axis_index(axis)
    rows = block.shape[0]
    got = [hop(block, axis, k) for k in (1, 3, 2)]
    out = jnp.zeros((4 * rows,) + block.shape[1:], block.dtype)
    for k, piece in zip((0, 1, 3, 2), [block] + got):
        out = lax.dynamic_update_slice_in_dim(out, piece, ((here - k) % 4) * rows, 0)
    return out


def summed_rows(value, first, second):
    part = scatter_sum(scatter_sum(value, first), second)
    return gather_rows(gather_rows(part, second), first)


def summed_small(value):
    for axis in ("x", Z):
        value = (value + hop(value, axis, 2)) + (hop(value, axis, 1) + hop(value, axis, -1))
    return value


def per_device(queries, keys, values, bias_u, bias_w, rel_table, out_weight, grad_out, doc_lengths):
    seg_len = queries.shape[1]
    half = out_weight.shape[0] // 2
    x, y, co, z = (lax.axis_index(a) for a in ("x", "y", "co", Z))
    memory_keys, memory_values = from_behind((keys[0], values[0]), CTX, 1)
    pieces_a = two_axes(out_weight[:half], "x", Z)
    pieces_b = two_axes(out_weight[half:], Z, "x")
    pieces_a = (pieces_a[0],) + pieces_a[1:]
    cot_own = stacked_ring(grad_out[0], "y")
    cot_side = lax.ppermute(cot_own, "co", [(0, 1), (1, 0)])

    def slice_of(dx, dz):
        px, pz = (x + dx) % 4, (z + dz) % 4
        return ((pz // 2) * 4 + px) * 2 + pz % 2

    ids_a = jnp.stack([slice_of(dx, dz) for dz in NEAR for dx in NEAR]).astype(jnp.int32)
    ids_b = jnp.stack([slice_of(dx, dz) for dx in NEAR for dz in NEAR]).astype(jnp.int32)
    blocks = jnp.stack([2 * ((y + dy) % 4) + c for c in (co, 1 - co) for dy in NEAR]).astype(jnp.int32)

    doc_ends = jnp.cumsum(doc_lengths[0])
    seg_start = lax.axis_index(CTX) * seg_len
    token = seg_start + jnp.arange(seg_len, dtype=jnp.int32)
    doc_start = jnp.sum(jnp.where(doc_ends[None, :] <= token[:, None], doc_lengths[0][None, :], 0), axis=1)
    start = (doc_start - (seg_start - seg_len)).astype(jnp.int32)[:, None]

    row_u, row_w = bias_u[None, :], bias_w[None, :]
    weights = weights_call(start, queries[0], memory_keys, keys[0], rel_table, row_u, row_w)
    outs = []
    for ids, pieces, first in ((ids_a, pieces_a, 0), (ids_b, pieces_b, 4)):
        grad_heads = project(ids, blocks, pieces, cot_own, cot_side)
        outs.append(grads_call(
            weights, grad_heads, queries[0], memory_keys, keys[0], memory_values, values[0],
            rel_table, row_u, row_w, h0=first, heads=4))
    done = []
    for part, (dq, dk_mem, dk_own, dv_mem, dv_own, table, biases) in enumerate(outs):
        back_keys, back_values = from_behind((dk_mem, dv_mem), CTX, -1)
        grad_keys = (dk_own + back_keys.astype(jnp.float32)).astype(jnp.bfloat16)
        grad_values = (dv_own + back_values.astype(jnp.float32)).astype(jnp.bfloat16)
        order = ("x", Z) if part == 0 else (Z, "x")
        grad_table = summed_rows(table, *order).astype(jnp.float32)
        done.append((dq, grad_keys, grad_values, grad_table, biases))
    dq, grad_keys, grad_values, grad_table, biases = (jnp.concatenate(pair, axis=1) for pair in zip(*done))
    return (dq[None], grad_keys[None], grad_values[None], grad_table, summed_small(biases))


def solution(mesh):
    torus = Mesh(mesh.devices.reshape(2, 4, 4, 2, 2), AXES)
    rows = P("zl", CTX, TP)
    placed = (rows, rows, rows, P(TP), P(TP), P(None, TP), P(TP, CTX_DP), rows, P("zl", None))
    return jax.shard_map(
        per_device,
        mesh=torus,
        in_specs=placed,
        out_specs=(rows, rows, rows, P(None, TP), P(None, TP)),
        check_vma=False,
    )
```
